32 devices in a mesh: tm: 8 (over y, x, core), space: 4 (over z).
Axes of the slice: x: 2, y: 2, z: 4, core: 2. Of those that a mesh axis runs over, the one named last changes fastest.
Arguments:
- tokens: bfloat16 [8, 1024, 512], P('tm', 'space'), may hold values from -6 to 6
- attn_gain: float32 [512], replicated, may hold values from 0.1 to 1.9
- cross_gain: float32 [512], replicated, may hold values from 0.1 to 1.9
- ffn_gain: float32 [512], replicated, may hold values from 0.1 to 1.9
- w_query: bfloat16 [512, 512], replicated, may hold values from -1 to 1
- w_key: bfloat16 [512, 512], replicated, may hold values from -1 to 1
- w_value: bfloat16 [512, 512], replicated, may hold values from -0.25 to 0.25
- w_attn_out: bfloat16 [512, 512], replicated, may hold values from -0.25 to 0.25
- w_cross_q: bfloat16 [512, 512], replicated, may hold values from -0.25 to 0.25
- w_cross_out: bfloat16 [512, 512], replicated, may hold values from -0.25 to 0.25
- w_in: bfloat16 [512, 2048], replicated, may hold values from -0.25 to 0.25
- w_out: bfloat16 [2048, 512], replicated, may hold values from -0.125 to 0.125
- hist_keys: bfloat16 [256, 96, 512], P('tm', 'space'), may hold values from -160 to 160
- hist_values: bfloat16 [256, 96, 512], P('tm', 'space'), may hold values from -12 to 12
- flags: int32 [8, 8], replicated, may hold values from 0 to 255, as said below
- tile_map: int32 [1024], P('space'), may hold values from 0 to 1023, as said below
Outputs:
- layer_out: float32 [8, 1024, 512], P(None, ('space', 'tm'))
The draws below stay inside these ranges and needn't reach their ends.
Inputs may be any that keep to these rules, and one draw needn't show every extreme that they name: `flags`: each row lists 8 different cached rounds; round h is held by owner h // 32; at most 2 entries of a row share an owner, and every row has an owner with exactly 2. `tile_map`: each aligned block of 256 entries is a permutation of the stabilizers of that block.
All inputs are finite; a program needn't handle non-finite values.
Results may differ from the reference program's by a relative error of at most 0.014.
The reference program's roundings to bfloat16 on the way count: a program that leaves them out, or rounds other values in their place, can miss the bound.
Values may be sent and summed in bfloat16 or wider, within the bound.
A program may use at most 128 MiB of HBM per device.

```python
import math
import jax
import jax.numpy as jnp
from jax import lax

D = 512
HEADS = 8
FF = 2048
SPAN = 8
S_DEV = 256
HIST_DEV = 32
STAB = 1024
WINDOW = 8
HIST = 256
KEEP_ALL = 96
FLAGS = 8


def draw_flags(key, part):
    owner_count = HIST // HIST_DEV
    pair_count = owner_count // 2
    hot_owner = jax.random.randint(jax.random.fold_in(key, 11), (owner_count,), 0, 4) == 0
    noise = jax.random.randint(jax.random.fold_in(key, 12), (WINDOW, owner_count), 0, 1 << 20)
    positions = jnp.arange(owner_count, dtype=jnp.int32)
    scores_int = (noise + jnp.where(hot_owner, 1 << 20, 0)[None, :]) * owner_count + positions[None, :]
    ranking = jnp.argsort(-scores_int, axis=1, stable=True)
    first_owner = ranking[:, 0::2]
    second_owner = ranking[:, 1::2]
    double = jax.random.randint(jax.random.fold_in(key, 13), (WINDOW, pair_count), 0, 2) == 1
    double = double | (jnp.arange(pair_count) == 0)[None, :]
    base_round = jax.random.randint(jax.random.fold_in(key, 14), (WINDOW, pair_count), 0, HIST_DEV - 1)
    slot_first = first_owner * HIST_DEV + base_round
    slot_second = jnp.where(double, first_owner * HIST_DEV + base_round + 1, second_owner * HIST_DEV + base_round)
    rounds = jnp.stack([slot_first, slot_second], axis=-1).reshape(WINDOW, owner_count)
    mixing = jax.random.randint(jax.random.fold_in(key, 15), (WINDOW, owner_count), 0, 1 << 20)
    shuffle = jnp.argsort(mixing * owner_count + positions[None, :], axis=1, stable=True)
    return jnp.take_along_axis(rounds, shuffle, axis=1).astype(jnp.int32)


def draw_tile_map(key, part):
    tile_count = STAB // S_DEV
    tile_keys = jax.random.split(jax.random.fold_in(key, 21), tile_count)
    permuted = jax.vmap(lambda tile_key: jax.random.permutation(tile_key, S_DEV))(tile_keys)
    starts = jnp.arange(tile_count, dtype=jnp.int32) * S_DEV
    return (permuted + starts[:, None]).reshape(STAB).astype(jnp.int32)


def draw_w_query(key, part):
    column_scale = jnp.exp(jax.random.uniform(jax.random.fold_in(key, 41), (1, D), jnp.float32, math.log(1.2), math.log(2.6)))
    base_entries = jax.random.normal(jax.random.fold_in(key, 42), (D, D), jnp.float32)
    return jnp.clip(base_entries * column_scale * (1.0 / math.sqrt(D)), -1.0, 1.0).astype(jnp.bfloat16)


def draw_w_key(key, part):
    column_scale = jnp.exp(jax.random.uniform(jax.random.fold_in(key, 51), (1, D), jnp.float32, math.log(1.2), math.log(2.6)))
    base_entries = jax.random.normal(jax.random.fold_in(key, 52), (D, D), jnp.float32)
    return jnp.clip(base_entries * column_scale * (1.0 / math.sqrt(D)), -1.0, 1.0).astype(jnp.bfloat16)


def draw_hist_keys(key, part):
    base_normal = jax.random.normal(jax.random.fold_in(key, 31), (HIST, KEEP_ALL, D), jnp.float32)
    return jnp.clip(base_normal * 1.5, -9.0, 9.0).astype(jnp.bfloat16)


def level_of(stream_key, shape, pieces, least, largest):
    loudness, own = 1.0, jax.random.fold_in(stream_key, 6)
    for dim, parts in pieces:
        steps = jnp.exp(jax.random.uniform(jax.random.fold_in(own, dim), (parts,), jnp.float32, least / len(pieces), largest / len(pieces)))
        loudness = loudness * jnp.repeat(steps, shape[dim] // parts).reshape([-1 if axis == dim else 1 for axis in range(len(shape))])
    return loudness


def bell_draw(key, extent, width, bound, cuts=(), kind=jnp.bfloat16):
    entries = width * jax.random.normal(key, extent, jnp.float32)
    if cuts:
        entries = entries * level_of(key, extent, cuts, -0.22, 0.18)
    return jnp.clip(entries, -bound, bound).astype(kind)


def setup_inputs(seed: int = 0) -> dict:
    key_list = jax.random.split(jax.random.key(seed), 17)
    return {
        "tokens": bell_draw(key_list[0], (WINDOW, STAB, D), 1.0, 6.0, ((0, 8), (1, 4))),
        "attn_gain": jnp.clip(1.0 + 0.18 * jax.random.normal(key_list[1], (D,), jnp.float32), 0.1, 1.9),
        "cross_gain": jnp.clip(1.0 + 0.18 * jax.random.normal(key_list[2], (D,), jnp.float32), 0.1, 1.9),
        "ffn_gain": jnp.clip(1.0 + 0.18 * jax.random.normal(key_list[3], (D,), jnp.float32), 0.1, 1.9),
        "w_query": draw_w_query(jax.random.fold_in(key_list[16], 71), 0),
        "w_key": draw_w_key(jax.random.fold_in(key_list[16], 71), 0),
        "w_value": bell_draw(key_list[6], (D, D), D ** -0.5, 0.25),
        "w_attn_out": bell_draw(key_list[7], (D, D), D ** -0.5, 0.25),
        "w_cross_q": bell_draw(key_list[8], (D, D), D ** -0.5, 0.25),
        "w_cross_out": bell_draw(key_list[9], (D, D), D ** -0.5, 0.25),
        "w_in": bell_draw(key_list[10], (D, FF), D ** -0.5, 0.25),
        "w_out": bell_draw(key_list[11], (FF, D), FF ** -0.5, 0.125),
        "hist_keys": draw_hist_keys(jax.random.fold_in(key_list[16], 71), 0),
        "hist_values": bell_draw(key_list[13], (HIST, KEEP_ALL, D), 2.0, 12.0, ((0, 8), (1, 4))),
        "flags": draw_flags(jax.random.fold_in(key_list[16], 71), 0),
        "tile_map": draw_tile_map(jax.random.fold_in(key_list[16], 71), 0),
    }


def rms_scale(values_in, gain_row):
    widened = values_in.astype(jnp.float32)
    return widened * lax.rsqrt(lax.optimization_barrier(jnp.mean(widened * widened, axis=-1, keepdims=True)) + 1e-06) * gain_row

def project(normed, weight):
    return jnp.dot(normed, weight, preferred_element_type=jnp.float32)

def attend(queries, keys_in, values_in, usable):
    row_count = queries.shape[0]
    key_count = keys_in.shape[0]
    head_size = queries.shape[1] // HEADS
    query_heads = queries.reshape(row_count, HEADS, head_size).transpose(1, 0, 2)
    key_heads = keys_in.reshape(key_count, HEADS, head_size).transpose(1, 0, 2)
    value_heads = values_in.reshape(key_count, HEADS, head_size).transpose(1, 0, 2)
    factor = 1.0 / math.sqrt(head_size)

    def one_head(triple):
        query_head, key_head, value_head = triple
        scores = jnp.dot(query_head, key_head.T, preferred_element_type=jnp.float32) * factor
        scores = jnp.where(usable[None, :], scores, -1e+30)
        weights = jax.nn.softmax(scores, axis=-1).astype(jnp.bfloat16)
        return jnp.dot(weights, value_head, preferred_element_type=jnp.float32)
    attended = lax.map(one_head, (query_heads, key_heads, value_heads))
    return attended.transpose(1, 0, 2).reshape(row_count, HEADS * head_size).astype(jnp.bfloat16)

def reference(tokens, attn_gain, cross_gain, ffn_gain, w_query, w_key, w_value, w_attn_out, w_cross_q, w_cross_out, w_in, w_out, hist_keys, hist_values, flags, tile_map):
    flattened = tokens.reshape(WINDOW * STAB, D)
    normed = rms_scale(flattened, attn_gain).astype(jnp.bfloat16)
    queries = project(normed, w_query).astype(jnp.bfloat16).reshape(WINDOW, STAB, D)
    keys_all = project(normed, w_key).astype(jnp.bfloat16).reshape(WINDOW, STAB, D)
    values_all = project(normed, w_value).astype(jnp.bfloat16).reshape(WINDOW, STAB, D)
    zero_rounds = jnp.zeros((SPAN - 1, STAB, D), jnp.bfloat16)
    keys_padded = jnp.concatenate([zero_rounds, keys_all], axis=0)
    values_padded = jnp.concatenate([zero_rounds, values_all], axis=0)
    tile_count = STAB // S_DEV
    offsets = jnp.arange(SPAN * S_DEV, dtype=jnp.int32) // S_DEV
    every_key = jnp.ones((FLAGS * KEEP_ALL,), dtype=jnp.bool_)

    def per_round(round_index):
        query_tiles = queries[round_index].reshape(tile_count, S_DEV, D)
        key_span = lax.dynamic_slice_in_dim(keys_padded, round_index, SPAN, 0)
        value_span = lax.dynamic_slice_in_dim(values_padded, round_index, SPAN, 0)
        key_tiles = key_span.reshape(SPAN, tile_count, S_DEV, D).transpose(1, 0, 2, 3).reshape(tile_count, SPAN * S_DEV, D)
        value_tiles = value_span.reshape(SPAN, tile_count, S_DEV, D).transpose(1, 0, 2, 3).reshape(tile_count, SPAN * S_DEV, D)
        usable = round_index - (SPAN - 1) + offsets >= 0

        def tile_attend(triple):
            return attend(triple[0], triple[1], triple[2], usable)
        attended = lax.map(tile_attend, (query_tiles, key_tiles, value_tiles)).reshape(STAB, D)
        residual = tokens[round_index].astype(jnp.float32) + project(attended, w_attn_out)
        normed_two = rms_scale(residual, cross_gain).astype(jnp.bfloat16)
        cross_queries = project(normed_two, w_cross_q).astype(jnp.bfloat16)
        round_flags = flags[round_index]
        cross_keys = hist_keys[round_flags].reshape(FLAGS * KEEP_ALL, D)
        cross_values = hist_values[round_flags].reshape(FLAGS * KEEP_ALL, D)
        cross_attended = attend(cross_queries, cross_keys, cross_values, every_key)
        residual_two = residual + project(cross_attended, w_cross_out)
        normed_three = rms_scale(residual_two, ffn_gain).astype(jnp.bfloat16)
        hidden = jax.nn.gelu(project(normed_three, w_in)).astype(jnp.bfloat16)
        result = residual_two + project(hidden, w_out)
        return result[tile_map]
    return lax.map(per_round, jnp.arange(WINDOW, dtype=jnp.int32))
```

```python
import functools
import math

import jax
import jax.numpy as jnp
from jax import lax
from jax.experimental import pallas as pl
from jax.experimental.pallas import tpu as pltpu
from jax.sharding import PartitionSpec as P

HEADS = 8
SPAN = 8
CAP = 2
EXTRA = 16
CHUNKS = 4
AHEAD = 4
TOKENS_AFTER = 0
ORDER = (1, 3, 4, 0, 0, 1, 1, 1, 1)
MESH = pl.DeviceIdType.MESH
F32 = jnp.float32
BF16 = jnp.bfloat16


def scaled(x, gain):
    return x * lax.rsqrt(jnp.mean(x * x, axis=-1, keepdims=True) + 1e-06) * gain


def dot(a, b):
    return jnp.dot(a, b, preferred_element_type=F32)


def low_half(shape):
    return lax.broadcasted_iota(jnp.int32, shape, 1) < shape[1] // 2


def stacked(q):
    low = low_half(q.shape)
    none = jnp.zeros_like(q)
    return jnp.concatenate([jnp.where(low, q, none), jnp.where(low, none, q)], axis=0)


def pair_scores(q, k):
    return lax.dot_general(k, q, (((1,), (1,)), ((), ())), preferred_element_type=F32)


def pair_attend(s, v_t, old):
    top = jnp.max(s, axis=0, keepdims=True)
    if old is not None:
        top = jnp.maximum(top, old[0])
        shrink = jnp.exp(old[0] - top)
    e = jnp.exp(s - top).astype(BF16)
    head, wide = v_t.shape[0] // 2, s.shape[1] // 2
    totals = []
    for half in range(2):
        cols = slice(half * wide, (half + 1) * wide)
        rows = jnp.concatenate([v_t[half * head:(half + 1) * head], jnp.ones((EXTRA, v_t.shape[1]), BF16)], axis=0)
        total = dot(rows, e[:, cols])
        if old is not None:
            total = total + old[1][half] * shrink[:, cols]
        totals.append(total)
    return top, totals


def averaged(total):
    head = total.shape[0] - EXTRA
    return total[:head] * (1.0 / total[head:head + 1])


def layer_kernel(
    tm_n, sp_n,
    flags_ref, tok_ref, map_ref, ga_ref, gc_ref, gf_ref, *rest,
):
    weights_hbm, rest = rest[:8], rest[8:]
    hist_hbm, (out_ref, *rest) = rest[:2], rest[2:]
    weights, rest = rest[:8], rest[8:]
    hist, rest = rest[:2], rest[2:]
    wq_ref, wk_ref, wv_ref, wo_ref, wcq_ref, wco_ref, win_ref, wout_ref = weights
    (
        w_sem, h_sem, send_ref, tok_buf, k_buf, vt_buf, wvt_buf, q2_buf, res_buf, res_in, att_out, att_in,
        top_buf, acc_buf, kv_all,
        own_sem, hs_sem, hr_sem, ts_sem, tr_sem, zs_sem, zr_sem, rs_sem, rr_sem, as_sem, ar_sem,
        *recv,
    ) = rest
    me = lax.axis_index("tm")
    tile = lax.axis_index("space")
    s_dev, width = tok_ref.shape
    head = width // HEADS
    factor = 1.0 / math.sqrt(head)
    part = s_dev // tm_n
    even = lax.rem(me, 2) == 0
    sibling = jnp.where(even, me + 1, me - 1)
    pairs = HEADS // 2
    wide = width // CHUNKS

    def peer(i):
        return lax.rem(me + i, tm_n)

    def hist_copy(c, i):
        return pltpu.make_async_remote_copy(
            src_ref=send_ref.at[c, peer(i)], dst_ref=recv[c].at[pl.ds(me * CAP, CAP)],
            send_sem=hs_sem.at[c, i], recv_sem=hr_sem.at[c, i],
            device_id={"tm": peer(i)}, device_id_type=MESH)

    def tok_copy(src, slot, to, sem):
        return pltpu.make_async_remote_copy(
            src_ref=src, dst_ref=tok_buf.at[slot],
            send_sem=ts_sem.at[sem], recv_sem=tr_sem.at[slot],
            device_id={"tm": to}, device_id_type=MESH)

    def tok_wait(slot):
        tok_copy(tok_ref, slot, sibling, 0).wait_recv()

    def hop(direction, step, c):
        if direction == 0:
            origin, to = tile - step, tile + 1
        else:
            origin, to = tile + step, tile - 1
        return pltpu.make_async_remote_copy(
            src_ref=kv_all.at[c, origin], dst_ref=kv_all.at[c, origin],
            send_sem=zs_sem.at[direction, step, c], recv_sem=zr_sem.at[direction, step, c],
            device_id={"space": to}, device_id_type=MESH)

    def hop_sends(direction, step):
        if direction == 0:
            return jnp.logical_and(tile - step >= 0, tile + 1 < sp_n)
        return jnp.logical_and(tile + step < sp_n, tile >= 1)

    def hop_start(step, c):
        for direction in range(2):
            @pl.when(hop_sends(direction, step))
            def _():
                hop(direction, step, c).start()

    def hop_arrived(step, c):
        @pl.when(tile - 1 - step >= 0)
        def _():
            hop(0, step, c).wait_recv()

        @pl.when(tile + 1 + step < sp_n)
        def _():
            hop(1, step, c).wait_recv()

    def res_copy(i):
        return pltpu.make_async_remote_copy(
            src_ref=res_buf.at[peer(i)], dst_ref=res_in.at[me],
            send_sem=rs_sem.at[i], recv_sem=rr_sem.at[i],
            device_id={"tm": peer(i)}, device_id_type=MESH)

    def att_copy(c, i):
        return pltpu.make_async_remote_copy(
            src_ref=att_out.at[c, peer(i)], dst_ref=att_in.at[c, me],
            send_sem=as_sem.at[c, i], recv_sem=ar_sem.at[c, i],
            device_id={"tm": peer(i)}, device_id_type=MESH)

    barrier = pltpu.get_barrier_semaphore()
    for i in range(1, tm_n):
        pl.semaphore_signal(barrier, inc=1, device_id={"tm": peer(i)}, device_id_type=MESH)

    @pl.when(tile >= 1)
    def _():
        pl.semaphore_signal(barrier, inc=1, device_id={"space": tile - 1}, device_id_type=MESH)

    @pl.when(tile + 1 < sp_n)
    def _():
        pl.semaphore_signal(barrier, inc=1, device_id={"space": tile + 1}, device_id_type=MESH)

    hist_in = [pltpu.make_async_copy(hist_hbm[i], hist[i], h_sem.at[i]) for i in range(2)]
    for copy in hist_in:
        copy.start()
    weight_in = [pltpu.make_async_copy(weights_hbm[i], weights[i], w_sem.at[i]) for i in range(8)]
    for copy in weight_in:
        copy.start()

    count = flags_ref.shape[1]
    kept = recv[0].shape[2]
    rounds_here = hist[0].shape[0]
    first_here = me * rounds_here

    def each(n, step, init):
        if n <= 8:
            for i in range(n):
                init = step(i, init)
            return init
        return lax.fori_loop(0, n, step, init)

    zero = jnp.int32(0)

    def pick(w):
        def look(j, state):
            first, second, seen = state
            local = flags_ref[w, j] - first_here
            here = jnp.logical_and(local >= 0, local < rounds_here)
            first = jnp.where(jnp.logical_and(here, seen == 0), local, first)
            second = jnp.where(jnp.logical_and(here, seen == 1), local, second)
            return first, second, seen + here.astype(jnp.int32)

        return each(count, look, (zero, zero, zero))[:2]

    def row_of(j):
        owner = lax.div(flags_ref[me, j], rounds_here)

        def rank_of(i, rank):
            same = jnp.logical_and(i < j, lax.div(flags_ref[me, i], rounds_here) == owner)
            return rank + same.astype(jnp.int32)

        return owner * CAP + each(count, rank_of, zero)

    picks = [pick(w) for w in range(tm_n)] if tm_n <= 8 else None
    found = [row_of(j) for j in range(count)] if count <= 8 else None

    def lanes_of(c):
        return pl.ds(c * wide, wide)

    def fill(c):
        def one(w, carry):
            for slot, local in enumerate(picks[w] if picks else pick(w)):
                for kind in range(2):
                    send_ref[c, w, slot, kind] = hist[kind][local, :, lanes_of(c)]
            return carry

        each(tm_n, one, 0)

    def compact(c):
        def one(i, carry):
            first, second = (found[2 * i], found[2 * i + 1]) if found else (row_of(2 * i), row_of(2 * i + 1))
            for kind in range(2):
                both = jnp.concatenate(
                    [recv[c][first, kind].astype(F32), recv[c][second, kind].astype(F32)], axis=0)
                at = i * 2 * kept
                at = at if isinstance(i, int) else pl.multiple_of(at, 2 * kept)
                kv_all[c, tile, kind, pl.ds(at, 2 * kept), :] = both.astype(BF16)
            return carry

        each(count // 2, one, 0)

    def own(c):
        return pltpu.make_async_copy(send_ref.at[c, me], recv[c].at[pl.ds(me * CAP, CAP)], own_sem.at[c])

    def hist_send(c):
        if c < CHUNKS:
            own(c).start()
            for i in range(1, tm_n):
                hist_copy(c, i).start()

    def keep_queries(q):
        q = (q * factor).astype(BF16)
        for pair in range(pairs):
            q2_buf[pair] = stacked(q[:, pair * 2 * head:(pair + 1) * 2 * head])

    spots = map_ref[...] - tile * s_dev
    chosen = (lax.broadcasted_iota(jnp.int32, (s_dev, s_dev), 0) == spots).astype(F32).astype(BF16)
    current = lax.dot_general(chosen, tok_ref[...], (((0,), (0,)), ((), ())), preferred_element_type=F32)
    res_buf[...] = current.reshape(res_buf.shape)
    for copy in hist_in:
        copy.wait()
    for c in range(CHUNKS):
        fill(c)
    near = (tile >= 1).astype(jnp.int32) + (tile + 1 < sp_n).astype(jnp.int32)
    pl.semaphore_wait(barrier, tm_n - 1 + near)

    for c in range(AHEAD):
        hist_send(c)
    for copy in weight_in[:3]:
        copy.wait()
    wvt_buf[...] = wv_ref[...].T
    current = res_buf[...].reshape(s_dev, width)
    keep_queries(dot(scaled(current, ga_ref[...]).astype(BF16), wq_ref[...]))

    def project(slot, tokens):
        normed = scaled(tokens.astype(F32), ga_ref[...]).astype(BF16)
        k_buf[slot * s_dev:(slot + 1) * s_dev, :] = dot(normed, wk_ref[...]).astype(BF16)
        values = lax.dot_general(wvt_buf[...], normed, (((1,), (1,)), ((), ())), preferred_element_type=F32)
        vt_buf[:, slot * s_dev:(slot + 1) * s_dev] = values.astype(BF16)

    def attend(slot, slots, first):
        rows = slice(slot * s_dev, (slot + slots) * s_dev)
        def scores(pair):
            return pair_scores(q2_buf[pair], k_buf[rows, pair * 2 * head:(pair + 1) * 2 * head])

        ready = scores(0)
        for pair in range(pairs):
            now = ready
            if pair + 1 < pairs:
                ready = scores(pair + 1)
            old = None if first else (top_buf[pair:pair + 1, :], (acc_buf[2 * pair], acc_buf[2 * pair + 1]))
            top, totals = pair_attend(now, vt_buf[pair * 2 * head:(pair + 1) * 2 * head, rows], old)
            top_buf[pair:pair + 1, :] = top
            acc_buf[2 * pair], acc_buf[2 * pair + 1] = totals

    far = jnp.logical_and(jnp.logical_not(even), me + 7 < tm_n)

    def send_tokens():
        @pl.when(even)
        def _():
            tok_copy(tok_ref, 1, sibling, 3).start()

        for k in range(1, 4):
            @pl.when(me + 2 * k < tm_n)
            def _():
                tok_copy(tok_ref, 2 * k, me + 2 * k, k - 1).start()

        @pl.when(far)
        def _():
            tok_copy(tok_ref, 1, me + 7, 4).start()

    def arrived(c):
        own(c).wait()
        for i in range(1, tm_n):
            hist_copy(c, i).wait_recv()
        hist_send(c + AHEAD)
        if c == TOKENS_AFTER:
            send_tokens()
        compact(c)
        hop_start(0, c)

    onward = [(step, c) for step in range(sp_n - 1) for c in range(CHUNKS)]

    def pass_on(n):
        for _ in range(n):
            if onward:
                step, c = onward.pop(0)
                if step == 0:
                    arrived(c)
                else:
                    hop_arrived(step - 1, c)
                    hop_start(step, c)

    def relayed(k):
        return tok_copy(tok_buf.at[2 * k], 2 * k + 1, sibling, 4 + k)

    def direct(k):
        @pl.when(me - 2 * k >= 0)
        def _():
            tok_wait(2 * k)
            relayed(k).start()
            project(2 * k, tok_buf[2 * k])

    def group(k):
        @pl.when(me - 2 * k >= 0)
        def _():
            tok_wait(2 * k + 1)
            project(2 * k + 1, tok_buf[2 * k + 1])
            attend(2 * k, 2, False)

    if TOKENS_AFTER < 0:
        send_tokens()
    project(0, tok_ref[...])
    plan = list(ORDER)
    pass_on(plan.pop(0))
    attend(0, 1, True)
    pass_on(plan.pop(0))

    @pl.when(jnp.logical_or(jnp.logical_not(even), me >= 7))
    def _():
        tok_wait(1)
        project(1, tok_buf[1])
        attend(1, 1, False)

    pass_on(plan.pop(0))
    for work in (direct, group):
        for k in range(1, 4):
            work(k)
            pass_on(plan.pop(0))

    for copy in weight_in[3:]:
        copy.wait()
    attended = jnp.concatenate([averaged(acc_buf[h]) for h in range(HEADS)], axis=0).astype(BF16)
    residual = res_buf[...].reshape(s_dev, width) + lax.dot_general(
        attended, wo_ref[...], (((0,), (0,)), ((), ())), preferred_element_type=F32)
    res_buf[...] = residual.reshape(res_buf.shape)
    for i in range(1, tm_n):
        res_copy(i).start()
    res_in[me] = res_buf[me]
    keep_queries(dot(scaled(residual, gc_ref[...]).astype(BF16), wcq_ref[...]))

    pass_on(len(onward))
    for c in range(CHUNKS):
        hop_arrived(sp_n - 2, c)
        parts = []
        for pair in range(c * pairs // CHUNKS, (c + 1) * pairs // CHUNKS):
            inner = pl.ds(pair * 2 * head - c * wide, 2 * head)
            k = kv_all[c, :, 0, :, inner]
            v = kv_all[c, :, 1, :, inner]
            flat = (k.shape[0] * k.shape[1], k.shape[2])
            k, v_t = k.reshape(flat), v.reshape(flat).T
            parts += [averaged(total) for total in pair_attend(pair_scores(q2_buf[pair], k), v_t, None)[1]]
        done = jnp.concatenate(parts, axis=0).T
        att_out[c] = done.reshape(tm_n, part, wide).astype(BF16)
        for i in range(1, tm_n):
            att_copy(c, i).start()
        att_in[c, me] = att_out[c, me]

    for i in range(1, tm_n):
        res_copy(i).wait_recv()
    for c in range(CHUNKS):
        for i in range(1, tm_n):
            att_copy(c, i).wait_recv()

    def flat_rows(x):
        if part % 16:
            return x.astype(F32).reshape(s_dev, x.shape[2]).astype(BF16)
        return x.reshape(s_dev, x.shape[2])

    attended = jnp.concatenate([flat_rows(att_in[c]) for c in range(CHUNKS)], axis=1)
    total = res_in[...].reshape(s_dev, width) + dot(attended, wco_ref[...])
    normed = scaled(total, gf_ref[...]).astype(BF16)
    hidden_n = win_ref.shape[1]
    chunk = 512
    for c in range(hidden_n // chunk):
        cols = pl.ds(c * chunk, chunk)
        hidden = jax.nn.gelu(dot(normed, win_ref[:, cols])).astype(BF16)
        total = total + dot(hidden, wout_ref[cols, :])
    out_ref[...] = total.reshape(out_ref.shape).astype(out_ref.dtype)

    @pl.when(even)
    def _():
        tok_copy(tok_ref, 1, sibling, 3).wait_send()

    for k in range(1, 4):
        @pl.when(me + 2 * k < tm_n)
        def _():
            tok_copy(tok_ref, 2 * k, me + 2 * k, k - 1).wait_send()

        @pl.when(me - 2 * k >= 0)
        def _():
            relayed(k).wait_send()

    @pl.when(far)
    def _():
        tok_copy(tok_ref, 1, me + 7, 4).wait_send()

    for c in range(CHUNKS):
        for i in range(1, tm_n):
            hist_copy(c, i).wait_send()
            att_copy(c, i).wait_send()
        for s in range(sp_n - 1):
            for direction in range(2):
                @pl.when(hop_sends(direction, s))
                def _():
                    hop(direction, s, c).wait_send()
    for i in range(1, tm_n):
        res_copy(i).wait_send()


def body(
    tm_n, sp_n,
    tokens, attn_gain, cross_gain, ffn_gain,
    w_query, w_key, w_value, w_attn_out, w_cross_q, w_cross_out, w_in, w_out,
    hist_keys, hist_values, flags, tile_map,
):
    _, s_dev, width = tokens.shape
    _, kept, _ = hist_keys.shape
    window, count = flags.shape
    smem = pl.BlockSpec(memory_space=pltpu.SMEM)
    vmem = pl.BlockSpec(memory_space=pltpu.VMEM)
    anywhere = pl.BlockSpec(memory_space=pl.ANY)
    dma = pltpu.SemaphoreType.DMA
    weights = (w_query, w_key, w_value, w_attn_out, w_cross_q, w_cross_out, w_in, w_out)
    got = count * kept
    wide = width // CHUNKS
    return pl.pallas_call(
        functools.partial(layer_kernel, tm_n, sp_n),
        out_shape=jax.ShapeDtypeStruct((tm_n, s_dev // tm_n, width), F32),
        in_specs=[smem] + [vmem] * 5 + [anywhere] * 10,
        out_specs=vmem,
        scratch_shapes=[pltpu.VMEM(w.shape, BF16) for w in weights] + [
            pltpu.VMEM(hist_keys.shape, BF16),
            pltpu.VMEM(hist_values.shape, BF16),
            dma((8,)), dma((2,)),
            pltpu.VMEM((CHUNKS, window, CAP, 2, kept, wide), BF16),
            pltpu.VMEM((SPAN, s_dev, width), BF16),
            pltpu.VMEM((SPAN * s_dev, width), BF16),
            pltpu.VMEM((width, SPAN * s_dev), BF16),
            pltpu.VMEM((width, width), BF16),
            pltpu.VMEM((HEADS // 2, 2 * s_dev, 2 * width // HEADS), BF16),
            pltpu.VMEM((tm_n, s_dev // tm_n, width), F32),
            pltpu.VMEM((tm_n, s_dev // tm_n, width), F32),
            pltpu.VMEM((CHUNKS, tm_n, s_dev // tm_n, wide), BF16),
            pltpu.VMEM((CHUNKS, tm_n, s_dev // tm_n, wide), BF16),
            pltpu.VMEM((HEADS // 2, 2 * s_dev), F32),
            pltpu.VMEM((HEADS, width // HEADS + EXTRA, s_dev), F32),
            pltpu.VMEM((CHUNKS, sp_n, 2, got, wide), BF16),
            dma((CHUNKS,)), dma((CHUNKS, tm_n)), dma((CHUNKS, tm_n)), dma((8,)), dma((SPAN,)),
            dma((2, sp_n, CHUNKS)), dma((2, sp_n, CHUNKS)), dma((tm_n,)), dma((tm_n,)),
            dma((CHUNKS, tm_n)), dma((CHUNKS, tm_n)),
        ] + [pltpu.VMEM((tm_n * CAP, 2, kept, wide), BF16) for _ in range(CHUNKS)],
        compiler_params=pltpu.CompilerParams(
            collective_id=0, has_side_effects=True, vmem_limit_bytes=58 * 1024 * 1024),
        name="layer",
    )(
        flags, tokens[0], tile_map.reshape(1, s_dev),
        attn_gain.reshape(1, width), cross_gain.reshape(1, width), ffn_gain.reshape(1, width),
        *weights, hist_keys, hist_values,
    )


def solution(mesh):
    placed = (
        (P("tm", "space", None),)
        + (P(),) * 11
        + (P("tm", "space", None), P("tm", "space", None), P(), P("space"))
    )
    return jax.shard_map(
        functools.partial(body, mesh.shape["tm"], mesh.shape["space"]),
        mesh=mesh, in_specs=placed, out_specs=P(None, ("space", "tm"), None), check_vma=False,
    )
```

```python
import functools
import math

import jax
import jax.numpy as jnp
from jax import lax
from jax.experimental import pallas as pl
from jax.experimental.pallas import tpu as pltpu
from jax.sharding import PartitionSpec as P

HEADS = 8
SPAN = 8
CAP = 2
EXTRA = 16
CHUNKS = 4
AHEAD = 4
TOKENS_AFTER = 0
ORDER = (1, 3, 4, 0, 0, 1, 1, 1, 1)
STEPS = ((0, 2), (0, 1), (1, 2), (0, 3), (1, 1), (1, 3))
MESH = pl.DeviceIdType.MESH
F32 = jnp.float32
BF16 = jnp.bfloat16


def scaled(x, gain):
    return x * lax.rsqrt(jnp.mean(x * x, axis=-1, keepdims=True) + 1e-06) * gain


def dot(a, b):
    return jnp.dot(a, b, preferred_element_type=F32)


def low_half(shape):
    return lax.broadcasted_iota(jnp.int32, shape, 1) < shape[1] // 2


def stacked(q):
    low = low_half(q.shape)
    none = jnp.zeros_like(q)
    return jnp.concatenate([jnp.where(low, q, none), jnp.where(low, none, q)], axis=0)


def pair_scores(q, k):
    return lax.dot_general(k, q, (((1,), (1,)), ((), ())), preferred_element_type=F32)


def pair_attend(s, v_t, old):
    top = jnp.max(s, axis=0, keepdims=True)
    if old is not None:
        top = jnp.maximum(top, old[0])
        shrink = jnp.exp(old[0] - top)
    e = jnp.exp(s - top).astype(BF16)
    head, wide = v_t.shape[0] // 2, s.shape[1] // 2
    totals = []
    for half in range(2):
        cols = slice(half * wide, (half + 1) * wide)
        rows = jnp.concatenate([v_t[half * head:(half + 1) * head], jnp.ones((EXTRA, v_t.shape[1]), BF16)], axis=0)
        total = dot(rows, e[:, cols])
        if old is not None:
            total = total + old[1][half] * shrink[:, cols]
        totals.append(total)
    return top, totals


def averaged(total):
    head = total.shape[0] - EXTRA
    return total[:head] * (1.0 / total[head:head + 1])


def layer_kernel(
    tm_n, sp_n,
    flags_ref, tok_ref, map_ref, ga_ref, gc_ref, gf_ref, *rest,
):
    weights_hbm, rest = rest[:8], rest[8:]
    hist_hbm, (out_ref, *rest) = rest[:2], rest[2:]
    weights, rest = rest[:8], rest[8:]
    hist, rest = rest[:2], rest[2:]
    wq_ref, wk_ref, wv_ref, wo_ref, wcq_ref, wco_ref, win_ref, wout_ref = weights
    (
        w_sem, h_sem, send_ref, tok_buf, k_buf, vt_buf, wvt_buf, q2_buf, res_buf, res_in, att_out, att_in,
        top_buf, acc_buf, kv_all,
        own_sem, hs_sem, hr_sem, ts_sem, tr_sem, zs_sem, zr_sem, rs_sem, rr_sem, as_sem, ar_sem,
        *recv,
    ) = rest
    me = lax.axis_index("tm")
    tile = lax.axis_index("space")
    s_dev, width = tok_ref.shape
    head = width // HEADS
    factor = 1.0 / math.sqrt(head)
    part = s_dev // tm_n
    even = lax.rem(me, 2) == 0
    sibling = jnp.where(even, me + 1, me - 1)
    pairs = HEADS // 2
    wide = width // CHUNKS

    def peer(i):
        return lax.rem(me + i, tm_n)

    def hist_copy(c, i):
        return pltpu.make_async_remote_copy(
            src_ref=send_ref.at[c, peer(i)], dst_ref=recv[c].at[pl.ds(me * CAP, CAP)],
            send_sem=hs_sem.at[c, i], recv_sem=hr_sem.at[c, i],
            device_id={"tm": peer(i)}, device_id_type=MESH)

    def tok_copy(src, slot, to, sem):
        return pltpu.make_async_remote_copy(
            src_ref=src, dst_ref=tok_buf.at[slot],
            send_sem=ts_sem.at[sem], recv_sem=tr_sem.at[slot],
            device_id={"tm": to}, device_id_type=MESH)

    def tok_wait(slot):
        tok_copy(tok_ref, slot, sibling, 0).wait_recv()

    def hop(direction, step, c):
        if direction == 0:
            origin, to = tile - step, tile + 1
        else:
            origin, to = tile + step, tile - 1
        return pltpu.make_async_remote_copy(
            src_ref=kv_all.at[c, origin], dst_ref=kv_all.at[c, origin],
            send_sem=zs_sem.at[direction, step, c], recv_sem=zr_sem.at[direction, step, c],
            device_id={"space": to}, device_id_type=MESH)

    def hop_sends(direction, step):
        if direction == 0:
            return jnp.logical_and(tile - step >= 0, tile + 1 < sp_n)
        return jnp.logical_and(tile + step < sp_n, tile >= 1)

    def hop_start(step, c):
        for direction in range(2):
            @pl.when(hop_sends(direction, step))
            def _():
                hop(direction, step, c).start()

    def hop_arrived(step, c):
        @pl.when(tile - 1 - step >= 0)
        def _():
            hop(0, step, c).wait_recv()

        @pl.when(tile + 1 + step < sp_n)
        def _():
            hop(1, step, c).wait_recv()

    def res_copy(i):
        return pltpu.make_async_remote_copy(
            src_ref=res_buf.at[peer(i)], dst_ref=res_in.at[me],
            send_sem=rs_sem.at[i], recv_sem=rr_sem.at[i],
            device_id={"tm": peer(i)}, device_id_type=MESH)

    def att_copy(c, i):
        return pltpu.make_async_remote_copy(
            src_ref=att_out.at[c, peer(i)], dst_ref=att_in.at[c, me],
            send_sem=as_sem.at[c, i], recv_sem=ar_sem.at[c, i],
            device_id={"tm": peer(i)}, device_id_type=MESH)

    barrier = pltpu.get_barrier_semaphore()
    for i in range(1, tm_n):
        pl.semaphore_signal(barrier, inc=1, device_id={"tm": peer(i)}, device_id_type=MESH)

    @pl.when(tile >= 1)
    def _():
        pl.semaphore_signal(barrier, inc=1, device_id={"space": tile - 1}, device_id_type=MESH)

    @pl.when(tile + 1 < sp_n)
    def _():
        pl.semaphore_signal(barrier, inc=1, device_id={"space": tile + 1}, device_id_type=MESH)

    hist_in = [pltpu.make_async_copy(hist_hbm[i], hist[i], h_sem.at[i]) for i in range(2)]
    for copy in hist_in:
        copy.start()
    weight_in = [pltpu.make_async_copy(weights_hbm[i], weights[i], w_sem.at[i]) for i in range(8)]
    for copy in weight_in:
        copy.start()

    count = flags_ref.shape[1]
    kept = recv[0].shape[2]
    rounds_here = hist[0].shape[0]
    first_here = me * rounds_here

    def each(n, step, init):
        if n <= 8:
            for i in range(n):
                init = step(i, init)
            return init
        return lax.fori_loop(0, n, step, init)

    zero = jnp.int32(0)

    def pick(w):
        def look(j, state):
            first, second, seen = state
            local = flags_ref[w, j] - first_here
            here = jnp.logical_and(local >= 0, local < rounds_here)
            first = jnp.where(jnp.logical_and(here, seen == 0), local, first)
            second = jnp.where(jnp.logical_and(here, seen == 1), local, second)
            return first, second, seen + here.astype(jnp.int32)

        return each(count, look, (zero, zero, zero))[:2]

    def row_of(j):
        owner = lax.div(flags_ref[me, j], rounds_here)

        def rank_of(i, rank):
            same = jnp.logical_and(i < j, lax.div(flags_ref[me, i], rounds_here) == owner)
            return rank + same.astype(jnp.int32)

        return owner * CAP + each(count, rank_of, zero)

    picks = [pick(w) for w in range(tm_n)] if tm_n <= 8 else None
    found = [row_of(j) for j in range(count)] if count <= 8 else None

    def lanes_of(c):
        return pl.ds(c * wide, wide)

    def fill(c):
        def one(w, carry):
            for slot, local in enumerate(picks[w] if picks else pick(w)):
                for kind in range(2):
                    send_ref[c, w, slot, kind] = hist[kind][local, :, lanes_of(c)]
            return carry

        each(tm_n, one, 0)

    def compact(c):
        def one(i, carry):
            first, second = (found[2 * i], found[2 * i + 1]) if found else (row_of(2 * i), row_of(2 * i + 1))
            for kind in range(2):
                both = jnp.concatenate(
                    [recv[c][first, kind].astype(F32), recv[c][second, kind].astype(F32)], axis=0)
                at = i * 2 * kept
                at = at if isinstance(i, int) else pl.multiple_of(at, 2 * kept)
                kv_all[c, tile, kind, pl.ds(at, 2 * kept), :] = both.astype(BF16)
            return carry

        each(count // 2, one, 0)

    def own(c):
        return pltpu.make_async_copy(send_ref.at[c, me], recv[c].at[pl.ds(me * CAP, CAP)], own_sem.at[c])

    def hist_send(c):
        if c < CHUNKS:
            own(c).start()
            for i in range(1, tm_n):
                hist_copy(c, i).start()

    def keep_queries(q):
        q = (q * factor).astype(BF16)
        for pair in range(pairs):
            q2_buf[pair] = stacked(q[:, pair * 2 * head:(pair + 1) * 2 * head])

    spots = map_ref[...] - tile * s_dev
    chosen = (lax.broadcasted_iota(jnp.int32, (s_dev, s_dev), 0) == spots).astype(F32).astype(BF16)
    current = lax.dot_general(chosen, tok_ref[...], (((0,), (0,)), ((), ())), preferred_element_type=F32)
    res_buf[...] = current.reshape(res_buf.shape)
    for copy in hist_in:
        copy.wait()
    for c in range(CHUNKS):
        fill(c)
    near = (tile >= 1).astype(jnp.int32) + (tile + 1 < sp_n).astype(jnp.int32)
    pl.semaphore_wait(barrier, tm_n - 1 + near)

    for c in range(AHEAD):
        hist_send(c)
    for copy in weight_in[:3]:
        copy.wait()
    wvt_buf[...] = wv_ref[...].T
    current = res_buf[...].reshape(s_dev, width)
    keep_queries(dot(scaled(current, ga_ref[...]).astype(BF16), wq_ref[...]))

    def project(slot, tokens):
        normed = scaled(tokens.astype(F32), ga_ref[...]).astype(BF16)
        k_buf[slot * s_dev:(slot + 1) * s_dev, :] = dot(normed, wk_ref[...]).astype(BF16)
        values = lax.dot_general(wvt_buf[...], normed, (((1,), (1,)), ((), ())), preferred_element_type=F32)
        vt_buf[:, slot * s_dev:(slot + 1) * s_dev] = values.astype(BF16)

    def attend(slot, slots, first):
        rows = slice(slot * s_dev, (slot + slots) * s_dev)
        def scores(pair):
            return pair_scores(q2_buf[pair], k_buf[rows, pair * 2 * head:(pair + 1) * 2 * head])

        ready = scores(0)
        for pair in range(pairs):
            now = ready
            if pair + 1 < pairs:
                ready = scores(pair + 1)
            old = None if first else (top_buf[pair:pair + 1, :], (acc_buf[2 * pair], acc_buf[2 * pair + 1]))
            top, totals = pair_attend(now, vt_buf[pair * 2 * head:(pair + 1) * 2 * head, rows], old)
            top_buf[pair:pair + 1, :] = top
            acc_buf[2 * pair], acc_buf[2 * pair + 1] = totals

    far = jnp.logical_and(jnp.logical_not(even), me + 7 < tm_n)

    odd = jnp.logical_not(even)
    chip_odd = lax.rem(me // 2, 2) == 1
    turns = jnp.logical_and(jnp.logical_and(odd, chip_odd), me + 4 < tm_n)

    first_sends = [
        (even, tok_copy(tok_ref, 1, sibling, 3)),
        (me + 4 < tm_n, tok_copy(tok_ref, 4, me + 4, 1)),
        (jnp.logical_and(me + 2 < tm_n, jnp.logical_not(turns)), tok_copy(tok_ref, 2, me + 2, 0)),
        (far, tok_copy(tok_ref, 1, me + 7, 4))]
    later_sends = {
        k: [(me - 2 * k >= 0, tok_copy(tok_buf.at[2 * k], 2 * k + 1, sibling, 4 + k))] for k in range(1, 4)}
    later_sends[1].append((
        jnp.logical_and(even, jnp.logical_and(me - 2 >= 0, me + 4 < tm_n)),
        tok_copy(tok_buf.at[2], 6, me + 4, 2)))
    later_sends[2].append((
        jnp.logical_and(odd, jnp.logical_and(me - 4 >= 0, me + 2 < tm_n)),
        tok_copy(tok_buf.at[4], 6, me + 2, 2)))
    later_sends[2].append((
        jnp.logical_and(jnp.logical_and(odd, chip_odd), me - 4 >= 0),
        tok_copy(tok_buf.at[4], 2, me - 2, 8)))

    def start_all(sends):
        for when, copy in sends:
            @pl.when(when)
            def _():
                copy.start()

    def send_tokens():
        start_all(first_sends)

    def arrived(c):
        own(c).wait()
        for i in range(1, tm_n):
            hist_copy(c, i).wait_recv()
        hist_send(c + AHEAD)
        if c == TOKENS_AFTER:
            send_tokens()
        compact(c)
        hop_start(0, c)

    onward = [(step, c) for step in range(sp_n - 1) for c in range(CHUNKS)]

    def pass_on(n):
        for _ in range(n):
            if onward:
                step, c = onward.pop(0)
                if step == 0:
                    arrived(c)
                else:
                    hop_arrived(step - 1, c)
                    hop_start(step, c)

    def direct(k):
        @pl.when(me - 2 * k >= 0)
        def _():
            tok_wait(2 * k)

        start_all(later_sends[k])

        @pl.when(me - 2 * k >= 0)
        def _():
            project(2 * k, tok_buf[2 * k])

    def group(k):
        @pl.when(me - 2 * k >= 0)
        def _():
            tok_wait(2 * k + 1)
            project(2 * k + 1, tok_buf[2 * k + 1])
            attend(2 * k, 2, False)

    if TOKENS_AFTER < 0:
        send_tokens()
    project(0, tok_ref[...])
    plan = list(ORDER)
    pass_on(plan.pop(0))
    attend(0, 1, True)
    pass_on(plan.pop(0))

    @pl.when(jnp.logical_or(jnp.logical_not(even), me >= 7))
    def _():
        tok_wait(1)
        project(1, tok_buf[1])
        attend(1, 1, False)

    pass_on(plan.pop(0))
    for work, k in STEPS:
        (direct, group)[work](k)
        pass_on(plan.pop(0))

    for copy in weight_in[3:]:
        copy.wait()
    attended = jnp.concatenate([averaged(acc_buf[h]) for h in range(HEADS)], axis=0).astype(BF16)
    residual = res_buf[...].reshape(s_dev, width) + lax.dot_general(
        attended, wo_ref[...], (((0,), (0,)), ((), ())), preferred_element_type=F32)
    res_buf[...] = residual.reshape(res_buf.shape)
    for i in range(1, tm_n):
        res_copy(i).start()
    res_in[me] = res_buf[me]
    keep_queries(dot(scaled(residual, gc_ref[...]).astype(BF16), wcq_ref[...]))

    pass_on(len(onward))
    for c in range(CHUNKS):
        hop_arrived(sp_n - 2, c)
        parts = []
        for pair in range(c * pairs // CHUNKS, (c + 1) * pairs // CHUNKS):
            inner = pl.ds(pair * 2 * head - c * wide, 2 * head)
            k = kv_all[c, :, 0, :, inner]
            v = kv_all[c, :, 1, :, inner]
            flat = (k.shape[0] * k.shape[1], k.shape[2])
            k, v_t = k.reshape(flat), v.reshape(flat).T
            parts += [averaged(total) for total in pair_attend(pair_scores(q2_buf[pair], k), v_t, None)[1]]
        done = jnp.concatenate(parts, axis=0).T
        att_out[c] = done.reshape(tm_n, part, wide).astype(BF16)
        for i in range(1, tm_n):
            att_copy(c, i).start()
        att_in[c, me] = att_out[c, me]

    for i in range(1, tm_n):
        res_copy(i).wait_recv()
    for c in range(CHUNKS):
        for i in range(1, tm_n):
            att_copy(c, i).wait_recv()

    def flat_rows(x):
        if part % 16:
            return x.astype(F32).reshape(s_dev, x.shape[2]).astype(BF16)
        return x.reshape(s_dev, x.shape[2])

    attended = jnp.concatenate([flat_rows(att_in[c]) for c in range(CHUNKS)], axis=1)
    total = res_in[...].reshape(s_dev, width) + dot(attended, wco_ref[...])
    normed = scaled(total, gf_ref[...]).astype(BF16)
    hidden_n = win_ref.shape[1]
    chunk = 512
    for c in range(hidden_n // chunk):
        cols = pl.ds(c * chunk, chunk)
        hidden = jax.nn.gelu(dot(normed, win_ref[:, cols])).astype(BF16)
        total = total + dot(hidden, wout_ref[cols, :])
    out_ref[...] = total.reshape(out_ref.shape).astype(out_ref.dtype)

    for when, copy in first_sends + later_sends[1] + later_sends[2] + later_sends[3]:
        @pl.when(when)
        def _():
            copy.wait_send()

    for c in range(CHUNKS):
        for i in range(1, tm_n):
            hist_copy(c, i).wait_send()
            att_copy(c, i).wait_send()
        for s in range(sp_n - 1):
            for direction in range(2):
                @pl.when(hop_sends(direction, s))
                def _():
                    hop(direction, s, c).wait_send()
    for i in range(1, tm_n):
        res_copy(i).wait_send()


def body(
    tm_n, sp_n,
    tokens, attn_gain, cross_gain, ffn_gain,
    w_query, w_key, w_value, w_attn_out, w_cross_q, w_cross_out, w_in, w_out,
    hist_keys, hist_values, flags, tile_map,
):
    _, s_dev, width = tokens.shape
    _, kept, _ = hist_keys.shape
    window, count = flags.shape
    smem = pl.BlockSpec(memory_space=pltpu.SMEM)
    vmem = pl.BlockSpec(memory_space=pltpu.VMEM)
    anywhere = pl.BlockSpec(memory_space=pl.ANY)
    dma = pltpu.SemaphoreType.DMA
    weights = (w_query, w_key, w_value, w_attn_out, w_cross_q, w_cross_out, w_in, w_out)
    got = count * kept
    wide = width // CHUNKS
    return pl.pallas_call(
        functools.partial(layer_kernel, tm_n, sp_n),
        out_shape=jax.ShapeDtypeStruct((tm_n, s_dev // tm_n, width), F32),
        in_specs=[smem] + [vmem] * 5 + [anywhere] * 10,
        out_specs=vmem,
        scratch_shapes=[pltpu.VMEM(w.shape, BF16) for w in weights] + [
            pltpu.VMEM(hist_keys.shape, BF16),
            pltpu.VMEM(hist_values.shape, BF16),
            dma((8,)), dma((2,)),
            pltpu.VMEM((CHUNKS, window, CAP, 2, kept, wide), BF16),
            pltpu.VMEM((SPAN, s_dev, width), BF16),
            pltpu.VMEM((SPAN * s_dev, width), BF16),
            pltpu.VMEM((width, SPAN * s_dev), BF16),
            pltpu.VMEM((width, width), BF16),
            pltpu.VMEM((HEADS // 2, 2 * s_dev, 2 * width // HEADS), BF16),
            pltpu.VMEM((tm_n, s_dev // tm_n, width), F32),
            pltpu.VMEM((tm_n, s_dev // tm_n, width), F32),
            pltpu.VMEM((CHUNKS, tm_n, s_dev // tm_n, wide), BF16),
            pltpu.VMEM((CHUNKS, tm_n, s_dev // tm_n, wide), BF16),
            pltpu.VMEM((HEADS // 2, 2 * s_dev), F32),
            pltpu.VMEM((HEADS, width // HEADS + EXTRA, s_dev), F32),
            pltpu.VMEM((CHUNKS, sp_n, 2, got, wide), BF16),
            dma((CHUNKS,)), dma((CHUNKS, tm_n)), dma((CHUNKS, tm_n)), dma((9,)), dma((SPAN,)),
            dma((2, sp_n, CHUNKS)), dma((2, sp_n, CHUNKS)), dma((tm_n,)), dma((tm_n,)),
            dma((CHUNKS, tm_n)), dma((CHUNKS, tm_n)),
        ] + [pltpu.VMEM((tm_n * CAP, 2, kept, wide), BF16) for _ in range(CHUNKS)],
        compiler_params=pltpu.CompilerParams(
            collective_id=0, has_side_effects=True, vmem_limit_bytes=58 * 1024 * 1024),
        name="layer",
    )(
        flags, tokens[0], tile_map.reshape(1, s_dev),
        attn_gain.reshape(1, width), cross_gain.reshape(1, width), ffn_gain.reshape(1, width),
        *weights, hist_keys, hist_values,
    )


def solution(mesh):
    placed = (
        (P("tm", "space", None),)
        + (P(),) * 11
        + (P("tm", "space", None), P("tm", "space", None), P(), P("space"))
    )
    return jax.shard_map(
        functools.partial(body, mesh.shape["tm"], mesh.shape["space"]),
        mesh=mesh, in_specs=placed, out_specs=P(None, ("space", "tm"), None), check_vma=False,
    )
```
